128 devices in a mesh: fsdp: 16 (over z_lo, y, core), tp: 8 (over x, z_hi).
Axes of the slice: x: 4, y: 4, z: 4 (z_hi: 2, z_lo: 2; z = z_hi * 2 + z_lo), core: 2. Of those that a mesh axis runs over, the one named last changes fastest.
Arguments:
- probe_states: bfloat16 [256, 16384], P('fsdp'), may hold values from -6 to 6
- wq_master: float32 [16384, 4096], P(('fsdp', 'tp')), may hold values from -1 to 1
- wq_first: float32 [16384, 4096], P(('fsdp', 'tp')), may hold values from -6 to 6
- wq_second: float32 [16384, 4096], P(('fsdp', 'tp')), may hold values from 0.25 to 4
- wq_grad: float32 [16384, 4096], P('fsdp', 'tp'), may hold values from -6 to 6
- wkv_master: float32 [16384, 512], P(('fsdp', 'tp')), may hold values from -0.046875 to 0.046875
- wkv_first: float32 [16384, 512], P(('fsdp', 'tp')), may hold values from -6 to 6
- wkv_second: float32 [16384, 512], P(('fsdp', 'tp')), may hold values from 0.25 to 4
- wkv_grad: float32 [16384, 512], P(('fsdp', 'tp')), may hold values from -6 to 6
Outputs:
- wq_updated: float32 [16384, 4096], P('fsdp', 'tp')
- wq_first_new: float32 [16384, 4096], P('fsdp', 'tp')
- wq_second_new: float32 [16384, 4096], P('fsdp', 'tp')
- wkv_updated: float32 [16384, 512], P(('fsdp', 'tp'))
- wkv_first_new: float32 [16384, 512], P(('fsdp', 'tp'))
- wkv_second_new: float32 [16384, 512], P(('fsdp', 'tp'))
- probe_query: bfloat16 [256, 4096], P('fsdp', 'tp')
- probe_keyvalue: bfloat16 [256, 512], replicated
The draws below stay inside these ranges and needn't reach their ends.
All inputs are finite; a program needn't handle non-finite values.
Results may differ from the reference program's by a relative error of at most 0.008.
Values may be sent and summed in bfloat16 or wider, within the bound.
A program may use at most 128 MiB of HBM per device.

```python
import math
import jax
import jax.numpy as jnp

D = 16384
QCOLS = 4096
KVCOLS = 512
TOKENS = 256


def optimizer_fields(key):
    shape = (D, QCOLS)
    key_first = jax.random.fold_in(key, 711)
    key_second = jax.random.fold_in(key, 712)
    key_grad = jax.random.fold_in(key, 713)
    moment_one = jnp.clip(jax.random.normal(key_first, shape, jnp.float32), -6.0, 6.0)
    gradient = jnp.clip(jax.random.normal(key_grad, shape, jnp.float32), -6.0, 6.0)
    lowest = math.log(0.25)
    highest = math.log(4.0)
    moment_two = jnp.exp(jax.random.uniform(key_second, shape, jnp.float32, lowest, highest))
    return (moment_one, moment_two, gradient)


def draw_wq_first(key, part):
    moment_one, moment_two, gradient = optimizer_fields(key)
    return moment_one


def draw_wq_second(key, part):
    moment_one, moment_two, gradient = optimizer_fields(key)
    return moment_two


def draw_wq_grad(key, part):
    moment_one, moment_two, gradient = optimizer_fields(key)
    return gradient


def draw_wq_master(key, part):
    shape = (D, QCOLS)
    key_master = jax.random.fold_in(key, 714)
    scale = 1.0 / math.sqrt(D)
    return jnp.clip(jax.random.normal(key_master, shape, jnp.float32), -6.0, 6.0) * scale


def level_of(stream_key, shape, cuts, low, top_value):
    def one(position, parts):
        heights = jax.random.uniform(jax.random.fold_in(jax.random.fold_in(stream_key, 6), position), (parts,), jnp.float32, low / len(cuts), top_value / len(cuts))
        return jnp.repeat(jnp.exp(heights), shape[position] // parts).reshape((-1,) + (1,) * (len(shape) - position - 1))

    factor_of = one(*cuts[0])
    for cut in cuts[1:]:
        factor_of = factor_of * one(*cut)
    return factor_of


def normal_values(own_key, extent, scale, most, split=(), kind=jnp.bfloat16):
    loudness = level_of(own_key, extent, split, -0.22, 0.18) if split else 1.0
    values = jax.random.normal(own_key, extent, jnp.float32) * scale * loudness
    return jnp.minimum(jnp.maximum(values, -most), most).astype(kind)


def setup_inputs(seed: int = 0) -> dict:
    key_list = jax.random.split(jax.random.key(seed), 10)
    probe_states = normal_values(key_list[0], (TOKENS, D), 1.0, 6.0, ((0, 16),))
    wq_master = draw_wq_master(jax.random.fold_in(key_list[9], 71), 0)
    wq_first = draw_wq_first(jax.random.fold_in(key_list[9], 71), 0)
    wq_second = draw_wq_second(jax.random.fold_in(key_list[9], 71), 0)
    wq_grad = draw_wq_grad(jax.random.fold_in(key_list[9], 71), 0)
    wkv_master = normal_values(key_list[5], (D, KVCOLS), D ** -0.5, 0.046875, ((0, 128),), jnp.float32)
    wkv_first = normal_values(key_list[6], (D, KVCOLS), 1.0, 6.0, ((0, 128),), jnp.float32)
    wkv_second = jnp.clip(jnp.exp(math.log(4.0) - 2.7725887 * jax.random.uniform(key_list[7], (D, KVCOLS), jnp.float32) ** level_of(key_list[7], (D, KVCOLS), ((0, 128),), -0.2, 0.2)), 0.25, 4.0)
    wkv_grad = normal_values(key_list[8], (D, KVCOLS), 1.0, 6.0, ((0, 128),), jnp.float32)
    return {"probe_states": probe_states, "wq_master": wq_master, "wq_first": wq_first, "wq_second": wq_second, "wq_grad": wq_grad, "wkv_master": wkv_master, "wkv_first": wkv_first, "wkv_second": wkv_second, "wkv_grad": wkv_grad}


BETA_ONE = 0.9
BETA_TWO = 0.95
LEARN_RATE = 0.001
EPSILON = 1e-08
CORRECT_ONE = 1.0 - math.exp(1000.0 * math.log(0.9))
CORRECT_TWO = 1.0 - math.exp(1000.0 * math.log(0.95))

def adam_step(master, first, second, grad):
    first_new = BETA_ONE * first + (1.0 - BETA_ONE) * grad
    second_new = BETA_TWO * second + (1.0 - BETA_TWO) * grad * grad
    update = first_new / CORRECT_ONE / (jnp.sqrt(second_new / CORRECT_TWO) + EPSILON)
    return (master - LEARN_RATE * update, first_new, second_new)

def reference(probe_states, wq_master, wq_first, wq_second, wq_grad, wkv_master, wkv_first, wkv_second, wkv_grad):
    wq_new, wq_mom, wq_var = adam_step(wq_master, wq_first, wq_second, wq_grad)
    wkv_new, wkv_mom, wkv_var = adam_step(wkv_master, wkv_first, wkv_second, wkv_grad)
    probe_query = jnp.dot(probe_states, wq_new.astype(jnp.bfloat16), preferred_element_type=jnp.float32).astype(jnp.bfloat16)
    probe_keyvalue = jnp.dot(probe_states, wkv_new.astype(jnp.bfloat16), preferred_element_type=jnp.float32).astype(jnp.bfloat16)
    return (wq_new, wq_mom, wq_var, wkv_new, wkv_mom, wkv_var, probe_query, probe_keyvalue)
```

```python
import math

import jax
import jax.numpy as jnp
from jax import lax
from jax.sharding import PartitionSpec as P

BETA_ONE = 0.9
BETA_TWO = 0.95
LEARN_RATE = 0.001
EPSILON = 1e-08
CORRECT_ONE = 1.0 - math.exp(1000.0 * math.log(0.9))
CORRECT_TWO = 1.0 - math.exp(1000.0 * math.log(0.95))


def adam_step(master, first, second, grad):
    first_new = BETA_ONE * first + (1.0 - BETA_ONE) * grad
    second_new = BETA_TWO * second + (1.0 - BETA_TWO) * grad * grad
    update = first_new / CORRECT_ONE / (jnp.sqrt(second_new / CORRECT_TWO) + EPSILON)
    return (master - LEARN_RATE * update, first_new, second_new)


def gather_rows(x, axis_name, size):
    copies = jnp.broadcast_to(x[None], (size,) + x.shape).reshape((size * x.shape[0],) + x.shape[1:])
    return lax.all_to_all(copies, axis_name, split_axis=0, concat_axis=0, tiled=True)


def scatter_sum_rows(x, axis_name, size):
    parts = lax.all_to_all(x, axis_name, split_axis=0, concat_axis=0, tiled=True)
    return parts.reshape((size, x.shape[0] // size) + x.shape[1:]).sum(axis=0)


def body(
    probe_states,
    wq_master,
    wq_first,
    wq_second,
    wq_grad,
    wkv_master,
    wkv_first,
    wkv_second,
    wkv_grad,
):
    fsdp = lax.axis_size("fsdp")
    tp = lax.axis_size("tp")
    columns = lax.all_to_all(probe_states, "fsdp", split_axis=1, concat_axis=0, tiled=True)
    wkv_new, wkv_mom, wkv_var = adam_step(wkv_master, wkv_first, wkv_second, wkv_grad)
    wkv_rows = gather_rows(wkv_new.astype(jnp.bfloat16), "tp", tp)
    kv_term = jnp.dot(columns, wkv_rows, preferred_element_type=jnp.float32)

    master, first, second = (
        lax.all_to_all(wq_master, "tp", split_axis=1, concat_axis=0, tiled=True),
        lax.all_to_all(wq_first, "tp", split_axis=1, concat_axis=0, tiled=True),
        lax.all_to_all(wq_second, "tp", split_axis=1, concat_axis=0, tiled=True),
    )
    wq_new, wq_mom, wq_var = adam_step(master, first, second, wq_grad)
    q_term = jnp.dot(columns, wq_new.astype(jnp.bfloat16), preferred_element_type=jnp.float32)

    sums = scatter_sum_rows(jnp.concatenate([q_term, kv_term], axis=1), "fsdp", fsdp)
    q_cols = q_term.shape[1]
    probe_query = sums[:, :q_cols].astype(jnp.bfloat16)
    probe_keyvalue = gather_rows(sums[:, q_cols:].astype(jnp.bfloat16), "fsdp", fsdp)
    return (wq_new, wq_mom, wq_var, wkv_new, wkv_mom, wkv_var, probe_query, probe_keyvalue)


def solution(mesh):
    return jax.shard_map(
        body,
        mesh=mesh,
        in_specs=(
            P("fsdp", None),
            P(("fsdp", "tp"), None),
            P(("fsdp", "tp"), None),
            P(("fsdp", "tp"), None),
            P("fsdp", "tp"),
            P(("fsdp", "tp"), None),
            P(("fsdp", "tp"), None),
            P(("fsdp", "tp"), None),
            P(("fsdp", "tp"), None),
        ),
        out_specs=(
            P("fsdp", "tp"),
            P("fsdp", "tp"),
            P("fsdp", "tp"),
            P(("fsdp", "tp"), None),
            P(("fsdp", "tp"), None),
            P(("fsdp", "tp"), None),
            P("fsdp", "tp"),
            P(),
        ),
        check_vma=False,
    )
```

```python
import math

import jax
import jax.numpy as jnp
from jax import lax
from jax.sharding import PartitionSpec as P

BETA_ONE = 0.9
BETA_TWO = 0.95
LEARN_RATE = 0.001
EPSILON = 1e-08
CORRECT_ONE = 1.0 - math.exp(1000.0 * math.log(0.9))
CORRECT_TWO = 1.0 - math.exp(1000.0 * math.log(0.95))


def adam_step(master, first, second, grad):
    first_new = BETA_ONE * first + (1.0 - BETA_ONE) * grad
    second_new = BETA_TWO * second + (1.0 - BETA_TWO) * grad * grad
    update = first_new / CORRECT_ONE / (jnp.sqrt(second_new / CORRECT_TWO) + EPSILON)
    return (master - LEARN_RATE * update, first_new, second_new)


def gather_rows(x, axis_name, size):
    copies = jnp.broadcast_to(x[None], (size,) + x.shape).reshape((size * x.shape[0],) + x.shape[1:])
    return lax.all_to_all(copies, axis_name, split_axis=0, concat_axis=0, tiled=True)


def scatter_sum_rows(x, axis_name, size):
    parts = lax.all_to_all(x, axis_name, split_axis=0, concat_axis=0, tiled=True)
    return parts.reshape((size, x.shape[0] // size) + x.shape[1:]).sum(axis=0)


def body(
    probe_states,
    wq_master,
    wq_first,
    wq_second,
    wq_grad,
    wkv_master,
    wkv_first,
    wkv_second,
    wkv_grad,
):
    fsdp = lax.axis_size("fsdp")
    columns = lax.all_to_all(probe_states, "fsdp", split_axis=1, concat_axis=0, tiled=True)
    wkv_new, wkv_mom, wkv_var = adam_step(wkv_master, wkv_first, wkv_second, wkv_grad)
    wkv_rows = lax.all_gather(wkv_new.astype(jnp.bfloat16), "tp", axis=0, tiled=True)
    kv_term = jnp.dot(columns, wkv_rows, preferred_element_type=jnp.float32)

    tp = lax.axis_size("tp")
    rows, cols = wq_master.shape
    pieces = [x.reshape(rows, tp, cols // tp).transpose(1, 0, 2) for x in (wq_master, wq_first, wq_second)]
    state = lax.all_to_all(jnp.concatenate(pieces, axis=1), "tp", split_axis=0, concat_axis=0, tiled=True)
    master, first, second = (state[:, k * rows:(k + 1) * rows].reshape(tp * rows, cols // tp) for k in range(3))
    wq_new, wq_mom, wq_var = adam_step(master, first, second, wq_grad)
    q_term = jnp.dot(columns, wq_new.astype(jnp.bfloat16), preferred_element_type=jnp.float32)

    sums = scatter_sum_rows(jnp.concatenate([q_term, kv_term], axis=1), "fsdp", fsdp)
    q_cols = q_term.shape[1]
    probe_query = sums[:, :q_cols].astype(jnp.bfloat16)
    probe_keyvalue = gather_rows(sums[:, q_cols:].astype(jnp.bfloat16), "fsdp", fsdp)
    return (wq_new, wq_mom, wq_var, wkv_new, wkv_mom, wkv_var, probe_query, probe_keyvalue)


def solution(mesh):
    return jax.shard_map(
        body,
        mesh=mesh,
        in_specs=(
            P("fsdp", None),
            P(("fsdp", "tp"), None),
            P(("fsdp", "tp"), None),
            P(("fsdp", "tp"), None),
            P("fsdp", "tp"),
            P(("fsdp", "tp"), None),
            P(("fsdp", "tp"), None),
            P(("fsdp", "tp"), None),
            P(("fsdp", "tp"), None),
        ),
        out_specs=(
            P("fsdp", "tp"),
            P("fsdp", "tp"),
            P("fsdp", "tp"),
            P(("fsdp", "tp"), None),
            P(("fsdp", "tp"), None),
            P(("fsdp", "tp"), None),
            P("fsdp", "tp"),
            P(),
        ),
        check_vma=False,
    )
```

```python
import math

import jax
import jax.numpy as jnp
from jax import lax
from jax.sharding import PartitionSpec as P


BETA_ONE = 0.9
BETA_TWO = 0.95
LEARN_RATE = 0.001
EPSILON = 1e-08
CORRECT_ONE = 1.0 - math.exp(1000.0 * math.log(0.9))
CORRECT_TWO = 1.0 - math.exp(1000.0 * math.log(0.95))


def adam_step(master, first, second, grad):
    first_new = BETA_ONE * first + (1.0 - BETA_ONE) * grad
    second_new = BETA_TWO * second + (1.0 - BETA_TWO) * grad * grad
    update = first_new / CORRECT_ONE / (jnp.sqrt(second_new / CORRECT_TWO) + EPSILON)
    return (master - LEARN_RATE * update, first_new, second_new)


def gather_rows(x, axis_name, size):
    copies = jnp.broadcast_to(x[None], (size,) + x.shape).reshape((size * x.shape[0],) + x.shape[1:])
    return lax.all_to_all(copies, axis_name, split_axis=0, concat_axis=0, tiled=True)


def scatter_sum_rows(x, axis_name, size):
    parts = lax.all_to_all(x, axis_name, split_axis=0, concat_axis=0, tiled=True)
    return parts.reshape((size, x.shape[0] // size) + x.shape[1:]).sum(axis=0)


def step(
    probe_states,
    wq_master,
    wq_first,
    wq_second,
    wq_grad,
    wkv_master,
    wkv_first,
    wkv_second,
    wkv_grad,
):
    fsdp = lax.axis_size("fsdp")
    columns = lax.all_to_all(probe_states, "fsdp", split_axis=1, concat_axis=0, tiled=True)
    wkv_new, wkv_mom, wkv_var = adam_step(wkv_master, wkv_first, wkv_second, wkv_grad)
    wkv_rows = lax.all_gather(wkv_new.astype(jnp.bfloat16), "tp", axis=0, tiled=True)
    kv_term = jnp.dot(columns, wkv_rows, preferred_element_type=jnp.float32)

    tp = lax.axis_size("tp")
    rows, cols = wq_master.shape
    pieces = [x.reshape(rows, tp, cols // tp).transpose(1, 0, 2) for x in (wq_master, wq_first, wq_second)]
    send = jnp.concatenate(pieces, axis=1)
    me = lax.axis_index("tp")
    got = [send[me]]
    for k in range(1, tp):
        block = lax.dynamic_index_in_dim(send, (me + k) % tp, 0, keepdims=False)
        got.append(lax.ppermute(block, "tp", [(i, (i + k) % tp) for i in range(tp)]))
    got = jnp.stack(got[::-1])
    state = lax.dynamic_slice_in_dim(jnp.concatenate([got, got]), tp - 1 - me, tp, 0)
    master, first, second = (state[:, k * rows:(k + 1) * rows].reshape(tp * rows, cols // tp) for k in range(3))
    wq_new, wq_mom, wq_var = adam_step(master, first, second, wq_grad)
    q_term = jnp.dot(columns, wq_new.astype(jnp.bfloat16), preferred_element_type=jnp.float32)

    sums = scatter_sum_rows(jnp.concatenate([q_term, kv_term], axis=1), "fsdp", fsdp)
    q_cols = q_term.shape[1]
    probe_query = sums[:, :q_cols].astype(jnp.bfloat16)
    probe_keyvalue = gather_rows(sums[:, q_cols:].astype(jnp.bfloat16), "fsdp", fsdp)
    return (wq_new, wq_mom, wq_var, wkv_new, wkv_mom, wkv_var, probe_query, probe_keyvalue)


def solution(mesh):
    return jax.shard_map(
        step,
        mesh=mesh,
        in_specs=(
            P("fsdp", None),
            P(("fsdp", "tp"), None),
            P(("fsdp", "tp"), None),
            P(("fsdp", "tp"), None),
            P("fsdp", "tp"),
            P(("fsdp", "tp"), None),
            P(("fsdp", "tp"), None),
            P(("fsdp", "tp"), None),
            P(("fsdp", "tp"), None),
        ),
        out_specs=(
            P("fsdp", "tp"),
            P("fsdp", "tp"),
            P("fsdp", "tp"),
            P(("fsdp", "tp"), None),
            P(("fsdp", "tp"), None),
            P(("fsdp", "tp"), None),
            P("fsdp", "tp"),
            P(),
        ),
        check_vma=False,
    )
```

```python
import math

import jax
import jax.numpy as jnp
from jax import lax
from jax.sharding import PartitionSpec as P


BETA_ONE = 0.9
BETA_TWO = 0.95
LEARN_RATE = 0.001
EPSILON = 1e-08
CORRECT_ONE = 1.0 - math.exp(1000.0 * math.log(0.9))
CORRECT_TWO = 1.0 - math.exp(1000.0 * math.log(0.95))


def adam_step(master, first, second, grad):
    first_new = BETA_ONE * first + (1.0 - BETA_ONE) * grad
    second_new = BETA_TWO * second + (1.0 - BETA_TWO) * grad * grad
    update = first_new / CORRECT_ONE / (jnp.sqrt(second_new / CORRECT_TWO) + EPSILON)
    return (master - LEARN_RATE * update, first_new, second_new)


def gather_rows(x, axis_name, size):
    copies = jnp.broadcast_to(x[None], (size,) + x.shape).reshape((size * x.shape[0],) + x.shape[1:])
    return lax.all_to_all(copies, axis_name, split_axis=0, concat_axis=0, tiled=True)


def scatter_sum_rows(x, axis_name, size):
    parts = lax.all_to_all(x, axis_name, split_axis=0, concat_axis=0, tiled=True)
    return parts.reshape((size, x.shape[0] // size) + x.shape[1:]).sum(axis=0)


def step(
    probe_states,
    wq_master,
    wq_first,
    wq_second,
    wq_grad,
    wkv_master,
    wkv_first,
    wkv_second,
    wkv_grad,
):
    fsdp = lax.axis_size("fsdp")
    me = lax.axis_index("fsdp")
    width = probe_states.shape[1] // fsdp
    got = [lax.dynamic_slice_in_dim(probe_states, me * width, width, 1)]
    for k in range(1, fsdp):
        block = lax.dynamic_slice_in_dim(probe_states, ((me + k) % fsdp) * width, width, 1)
        got.append(lax.ppermute(block, "fsdp", [(i, (i + k) % fsdp) for i in range(fsdp)]))
    got = jnp.stack(got[::-1])
    columns = lax.dynamic_slice_in_dim(jnp.concatenate([got, got]), fsdp - 1 - me, fsdp, 0)
    columns = columns.reshape(fsdp * probe_states.shape[0], width)
    wkv_new, wkv_mom, wkv_var = adam_step(wkv_master, wkv_first, wkv_second, wkv_grad)
    wkv_rows = lax.all_gather(wkv_new.astype(jnp.bfloat16), "tp", axis=0, tiled=True)
    kv_term = jnp.dot(columns, wkv_rows, preferred_element_type=jnp.float32)

    tp = lax.axis_size("tp")
    rows, cols = wq_master.shape
    pieces = [x.reshape(rows, tp, cols // tp).transpose(1, 0, 2) for x in (wq_master, wq_first, wq_second)]
    state = lax.all_to_all(jnp.concatenate(pieces, axis=1), "tp", split_axis=0, concat_axis=0, tiled=True)
    master, first, second = (state[:, k * rows:(k + 1) * rows].reshape(tp * rows, cols // tp) for k in range(3))
    wq_new, wq_mom, wq_var = adam_step(master, first, second, wq_grad)
    q_term = jnp.dot(columns, wq_new.astype(jnp.bfloat16), preferred_element_type=jnp.float32)

    sums = scatter_sum_rows(jnp.concatenate([q_term, kv_term], axis=1), "fsdp", fsdp)
    q_cols = q_term.shape[1]
    probe_query = sums[:, :q_cols].astype(jnp.bfloat16)
    probe_keyvalue = gather_rows(sums[:, q_cols:].astype(jnp.bfloat16), "fsdp", fsdp)
    return (wq_new, wq_mom, wq_var, wkv_new, wkv_mom, wkv_var, probe_query, probe_keyvalue)


def solution(mesh):
    return jax.shard_map(
        step,
        mesh=mesh,
        in_specs=(
            P("fsdp", None),
            P(("fsdp", "tp"), None),
            P(("fsdp", "tp"), None),
            P(("fsdp", "tp"), None),
            P("fsdp", "tp"),
            P(("fsdp", "tp"), None),
            P(("fsdp", "tp"), None),
            P(("fsdp", "tp"), None),
            P(("fsdp", "tp"), None),
        ),
        out_specs=(
            P("fsdp", "tp"),
            P("fsdp", "tp"),
            P("fsdp", "tp"),
            P(("fsdp", "tp"), None),
            P(("fsdp", "tp"), None),
            P(("fsdp", "tp"), None),
            P("fsdp", "tp"),
            P(),
        ),
        check_vma=False,
    )
```

```python
import math

import jax
import jax.numpy as jnp
from jax import lax
from jax.sharding import PartitionSpec as P


BETA_ONE = 0.9
BETA_TWO = 0.95
LEARN_RATE = 0.001
EPSILON = 1e-08
CORRECT_ONE = 1.0 - math.exp(1000.0 * math.log(0.9))
CORRECT_TWO = 1.0 - math.exp(1000.0 * math.log(0.95))


def adam_step(master, first, second, grad):
    first_new = BETA_ONE * first + (1.0 - BETA_ONE) * grad
    second_new = BETA_TWO * second + (1.0 - BETA_TWO) * grad * grad
    update = first_new / CORRECT_ONE / (jnp.sqrt(second_new / CORRECT_TWO) + EPSILON)
    return (master - LEARN_RATE * update, first_new, second_new)


def gather_rows(x, axis_name, size):
    copies = jnp.broadcast_to(x[None], (size,) + x.shape).reshape((size * x.shape[0],) + x.shape[1:])
    return lax.all_to_all(copies, axis_name, split_axis=0, concat_axis=0, tiled=True)


def scatter_sum_rows(x, axis_name, size):
    parts = lax.all_to_all(x, axis_name, split_axis=0, concat_axis=0, tiled=True)
    return parts.reshape((size, x.shape[0] // size) + x.shape[1:]).sum(axis=0)


def step(
    probe_states,
    wq_master,
    wq_first,
    wq_second,
    wq_grad,
    wkv_master,
    wkv_first,
    wkv_second,
    wkv_grad,
):
    fsdp = lax.axis_size("fsdp")
    me = lax.axis_index("fsdp")
    width = probe_states.shape[1] // fsdp
    got = [lax.dynamic_slice_in_dim(probe_states, me * width, width, 1)]
    for k in range(1, fsdp):
        block = lax.dynamic_slice_in_dim(probe_states, ((me + k) % fsdp) * width, width, 1)
        got.append(lax.ppermute(block, "fsdp", [(i, (i + k) % fsdp) for i in range(fsdp)]))
    got = jnp.stack(got[::-1])
    columns = lax.dynamic_slice_in_dim(jnp.concatenate([got, got]), fsdp - 1 - me, fsdp, 0)
    columns = columns.reshape(fsdp * probe_states.shape[0], width)
    wkv_new, wkv_mom, wkv_var = adam_step(wkv_master, wkv_first, wkv_second, wkv_grad)
    tp = lax.axis_size("tp")
    me_tp = lax.axis_index("tp")
    wkv_low = wkv_new.astype(jnp.bfloat16)
    rows_kv = [wkv_low]
    for k in range(1, tp):
        rows_kv.append(lax.ppermute(wkv_low, "tp", [(i, (i + k) % tp) for i in range(tp)]))
    rows_kv = jnp.stack(rows_kv[::-1])
    wkv_rows = lax.dynamic_slice_in_dim(jnp.concatenate([rows_kv, rows_kv]), tp - 1 - me_tp, tp, 0)
    wkv_rows = wkv_rows.reshape(tp * wkv_low.shape[0], wkv_low.shape[1])
    kv_term = jnp.dot(columns, wkv_rows, preferred_element_type=jnp.float32)

    rows, cols = wq_master.shape
    pieces = [x.reshape(rows, tp, cols // tp).transpose(1, 0, 2) for x in (wq_master, wq_first, wq_second)]
    state = lax.all_to_all(jnp.concatenate(pieces, axis=1), "tp", split_axis=0, concat_axis=0, tiled=True)
    master, first, second = (state[:, k * rows:(k + 1) * rows].reshape(tp * rows, cols // tp) for k in range(3))
    wq_new, wq_mom, wq_var = adam_step(master, first, second, wq_grad)
    q_term = jnp.dot(columns, wq_new.astype(jnp.bfloat16), preferred_element_type=jnp.float32)

    sums = scatter_sum_rows(jnp.concatenate([q_term, kv_term], axis=1), "fsdp", fsdp)
    q_cols = q_term.shape[1]
    probe_query = sums[:, :q_cols].astype(jnp.bfloat16)
    probe_keyvalue = gather_rows(sums[:, q_cols:].astype(jnp.bfloat16), "fsdp", fsdp)
    return (wq_new, wq_mom, wq_var, wkv_new, wkv_mom, wkv_var, probe_query, probe_keyvalue)


def solution(mesh):
    return jax.shard_map(
        step,
        mesh=mesh,
        in_specs=(
            P("fsdp", None),
            P(("fsdp", "tp"), None),
            P(("fsdp", "tp"), None),
            P(("fsdp", "tp"), None),
            P("fsdp", "tp"),
            P(("fsdp", "tp"), None),
            P(("fsdp", "tp"), None),
            P(("fsdp", "tp"), None),
            P(("fsdp", "tp"), None),
        ),
        out_specs=(
            P("fsdp", "tp"),
            P("fsdp", "tp"),
            P("fsdp", "tp"),
            P(("fsdp", "tp"), None),
            P(("fsdp", "tp"), None),
            P(("fsdp", "tp"), None),
            P("fsdp", "tp"),
            P(),
        ),
        check_vma=False,
    )
```

```python
import math

import jax
import jax.numpy as jnp
from jax import lax
from jax.sharding import PartitionSpec as P


BETA_ONE = 0.9
BETA_TWO = 0.95
LEARN_RATE = 0.001
EPSILON = 1e-08
CORRECT_ONE = 1.0 - math.exp(1000.0 * math.log(0.9))
CORRECT_TWO = 1.0 - math.exp(1000.0 * math.log(0.95))


def adam_step(master, first, second, grad):
    first_new = BETA_ONE * first + (1.0 - BETA_ONE) * grad
    second_new = BETA_TWO * second + (1.0 - BETA_TWO) * grad * grad
    update = first_new / CORRECT_ONE / (jnp.sqrt(second_new / CORRECT_TWO) + EPSILON)
    return (master - LEARN_RATE * update, first_new, second_new)


def gather_rows(x, axis_name, size):
    copies = jnp.broadcast_to(x[None], (size,) + x.shape).reshape((size * x.shape[0],) + x.shape[1:])
    return lax.all_to_all(copies, axis_name, split_axis=0, concat_axis=0, tiled=True)


def scatter_sum_rows(x, axis_name, size):
    parts = lax.all_to_all(x, axis_name, split_axis=0, concat_axis=0, tiled=True)
    return parts.reshape((size, x.shape[0] // size) + x.shape[1:]).sum(axis=0)


def step(
    probe_states,
    wq_master,
    wq_first,
    wq_second,
    wq_grad,
    wkv_master,
    wkv_first,
    wkv_second,
    wkv_grad,
):
    fsdp = lax.axis_size("fsdp")
    me = lax.axis_index("fsdp")
    width = probe_states.shape[1] // fsdp
    got = [lax.dynamic_slice_in_dim(probe_states, me * width, width, 1)]
    for k in range(1, fsdp):
        block = lax.dynamic_slice_in_dim(probe_states, ((me + k) % fsdp) * width, width, 1)
        got.append(lax.ppermute(block, "fsdp", [(i, (i + k) % fsdp) for i in range(fsdp)]))
    got = jnp.stack(got[::-1])
    columns = lax.dynamic_slice_in_dim(jnp.concatenate([got, got]), fsdp - 1 - me, fsdp, 0)
    columns = columns.reshape(fsdp * probe_states.shape[0], width)
    wkv_new, wkv_mom, wkv_var = adam_step(wkv_master, wkv_first, wkv_second, wkv_grad)
    tp = lax.axis_size("tp")
    me_tp = lax.axis_index("tp")
    wkv_low = wkv_new.astype(jnp.bfloat16)
    rows_kv = [wkv_low]
    for k in range(1, tp):
        rows_kv.append(lax.ppermute(wkv_low, "tp", [(i, (i + k) % tp) for i in range(tp)]))
    rows_kv = jnp.stack(rows_kv[::-1])
    wkv_rows = lax.dynamic_slice_in_dim(jnp.concatenate([rows_kv, rows_kv]), tp - 1 - me_tp, tp, 0)
    wkv_rows = wkv_rows.reshape(tp * wkv_low.shape[0], wkv_low.shape[1])
    kv_term = jnp.dot(columns, wkv_rows, preferred_element_type=jnp.float32)
    kv_sums = scatter_sum_rows(kv_term, "fsdp", fsdp)
    probe_keyvalue = gather_rows(kv_sums.astype(jnp.bfloat16), "fsdp", fsdp)

    rows, cols = wq_master.shape
    pieces = [x.reshape(rows, tp, cols // tp).transpose(1, 0, 2) for x in (wq_master, wq_first, wq_second)]
    state = lax.all_to_all(jnp.concatenate(pieces, axis=1), "tp", split_axis=0, concat_axis=0, tiled=True)
    master, first, second = (state[:, k * rows:(k + 1) * rows].reshape(tp * rows, cols // tp) for k in range(3))
    wq_new, wq_mom, wq_var = adam_step(master, first, second, wq_grad)
    q_term = jnp.dot(columns, wq_new.astype(jnp.bfloat16), preferred_element_type=jnp.float32)

    probe_query = scatter_sum_rows(q_term, "fsdp", fsdp).astype(jnp.bfloat16)
    return (wq_new, wq_mom, wq_var, wkv_new, wkv_mom, wkv_var, probe_query, probe_keyvalue)


def solution(mesh):
    return jax.shard_map(
        step,
        mesh=mesh,
        in_specs=(
            P("fsdp", None),
            P(("fsdp", "tp"), None),
            P(("fsdp", "tp"), None),
            P(("fsdp", "tp"), None),
            P("fsdp", "tp"),
            P(("fsdp", "tp"), None),
            P(("fsdp", "tp"), None),
            P(("fsdp", "tp"), None),
            P(("fsdp", "tp"), None),
        ),
        out_specs=(
            P("fsdp", "tp"),
            P("fsdp", "tp"),
            P("fsdp", "tp"),
            P(("fsdp", "tp"), None),
            P(("fsdp", "tp"), None),
            P(("fsdp", "tp"), None),
            P("fsdp", "tp"),
            P(),
        ),
        check_vma=False,
    )
```

```python
import math

import jax
import jax.numpy as jnp
from jax import lax
from jax.sharding import PartitionSpec as P


BETA_ONE = 0.9
BETA_TWO = 0.95
LEARN_RATE = 0.001
EPSILON = 1e-08
CORRECT_ONE = 1.0 - math.exp(1000.0 * math.log(0.9))
CORRECT_TWO = 1.0 - math.exp(1000.0 * math.log(0.95))


def adam_step(master, first, second, grad):
    first_new = BETA_ONE * first + (1.0 - BETA_ONE) * grad
    second_new = BETA_TWO * second + (1.0 - BETA_TWO) * grad * grad
    update = first_new / CORRECT_ONE / (jnp.sqrt(second_new / CORRECT_TWO) + EPSILON)
    return (master - LEARN_RATE * update, first_new, second_new)


def gather_rows(x, axis_name, size):
    copies = jnp.broadcast_to(x[None], (size,) + x.shape).reshape((size * x.shape[0],) + x.shape[1:])
    return lax.all_to_all(copies, axis_name, split_axis=0, concat_axis=0, tiled=True)


def scatter_sum_rows(x, axis_name, size):
    parts = lax.all_to_all(x, axis_name, split_axis=0, concat_axis=0, tiled=True)
    return parts.reshape((size, x.shape[0] // size) + x.shape[1:]).sum(axis=0)


def step(
    probe_states,
    wq_master,
    wq_first,
    wq_second,
    wq_grad,
    wkv_master,
    wkv_first,
    wkv_second,
    wkv_grad,
):
    fsdp = lax.axis_size("fsdp")
    me = lax.axis_index("fsdp")
    width = probe_states.shape[1] // fsdp
    got = [lax.dynamic_slice_in_dim(probe_states, me * width, width, 1)]
    for k in range(1, fsdp):
        block = lax.dynamic_slice_in_dim(probe_states, ((me + k) % fsdp) * width, width, 1)
        got.append(lax.ppermute(block, "fsdp", [(i, (i + k) % fsdp) for i in range(fsdp)]))
    got = jnp.stack(got[::-1])
    columns = lax.dynamic_slice_in_dim(jnp.concatenate([got, got]), fsdp - 1 - me, fsdp, 0)
    columns = columns.reshape(fsdp * probe_states.shape[0], width)
    wkv_new, wkv_mom, wkv_var = adam_step(wkv_master, wkv_first, wkv_second, wkv_grad)
    tp = lax.axis_size("tp")
    me_tp = lax.axis_index("tp")
    wkv_low = wkv_new.astype(jnp.bfloat16)
    slice_kv = wkv_low.shape[1] // tp
    rows_kv = [lax.dynamic_slice_in_dim(wkv_low, me_tp * slice_kv, slice_kv, 1)]
    for k in range(1, tp):
        block = lax.dynamic_slice_in_dim(wkv_low, ((me_tp + k) % tp) * slice_kv, slice_kv, 1)
        rows_kv.append(lax.ppermute(block, "tp", [(i, (i + k) % tp) for i in range(tp)]))
    rows_kv = jnp.stack(rows_kv[::-1])
    wkv_rows = lax.dynamic_slice_in_dim(jnp.concatenate([rows_kv, rows_kv]), tp - 1 - me_tp, tp, 0)
    wkv_rows = wkv_rows.reshape(tp * wkv_low.shape[0], slice_kv)
    kv_term = jnp.dot(columns, wkv_rows, preferred_element_type=jnp.float32)

    rows, cols = wq_master.shape
    pieces = [x.reshape(rows, tp, cols // tp).transpose(1, 0, 2) for x in (wq_master, wq_first, wq_second)]
    state = lax.all_to_all(jnp.concatenate(pieces, axis=1), "tp", split_axis=0, concat_axis=0, tiled=True)
    master, first, second = (state[:, k * rows:(k + 1) * rows].reshape(tp * rows, cols // tp) for k in range(3))
    wq_new, wq_mom, wq_var = adam_step(master, first, second, wq_grad)
    q_term = jnp.dot(columns, wq_new.astype(jnp.bfloat16), preferred_element_type=jnp.float32)

    sums = scatter_sum_rows(jnp.concatenate([q_term, kv_term], axis=1), "fsdp", fsdp)
    q_cols = q_term.shape[1]
    probe_query = sums[:, :q_cols].astype(jnp.bfloat16)
    kv_block = sums[:, q_cols:].astype(jnp.bfloat16)
    kv_all = gather_rows(kv_block, ("fsdp", "tp"), fsdp * tp)
    tokens = kv_block.shape[0]
    kv_all = kv_all.reshape(fsdp, tp, tokens, slice_kv).transpose(0, 2, 1, 3)
    probe_keyvalue = kv_all.reshape(fsdp * tokens, tp * slice_kv)
    return (wq_new, wq_mom, wq_var, wkv_new, wkv_mom, wkv_var, probe_query, probe_keyvalue)


def solution(mesh):
    return jax.shard_map(
        step,
        mesh=mesh,
        in_specs=(
            P("fsdp", None),
            P(("fsdp", "tp"), None),
            P(("fsdp", "tp"), None),
            P(("fsdp", "tp"), None),
            P("fsdp", "tp"),
            P(("fsdp", "tp"), None),
            P(("fsdp", "tp"), None),
            P(("fsdp", "tp"), None),
            P(("fsdp", "tp"), None),
        ),
        out_specs=(
            P("fsdp", "tp"),
            P("fsdp", "tp"),
            P("fsdp", "tp"),
            P(("fsdp", "tp"), None),
            P(("fsdp", "tp"), None),
            P(("fsdp", "tp"), None),
            P("fsdp", "tp"),
            P(),
        ),
        check_vma=False,
    )
```

```python
import math

import jax
import jax.numpy as jnp
from jax import lax
from jax.experimental import pallas as pl
from jax.sharding import PartitionSpec as P


BETA_ONE = 0.9
BETA_TWO = 0.95
LEARN_RATE = 0.001
EPSILON = 1e-08
CORRECT_ONE = 1.0 - math.exp(1000.0 * math.log(0.9))
CORRECT_TWO = 1.0 - math.exp(1000.0 * math.log(0.95))


def adam_step(master, first, second, grad):
    first_new = BETA_ONE * first + (1.0 - BETA_ONE) * grad
    second_new = BETA_TWO * second + (1.0 - BETA_TWO) * grad * grad
    update = first_new / CORRECT_ONE / (jnp.sqrt(second_new / CORRECT_TWO) + EPSILON)
    return (master - LEARN_RATE * update, first_new, second_new)


def adam_kernel(state_ref, grad_ref, master_out, first_out, second_out, low_out):
    per, rows = state_ref.shape[0], grad_ref.shape[0] // state_ref.shape[0]
    for j in range(per):
        out = pl.ds(j * rows, rows)
        new, first_new, second_new = adam_step(
            state_ref[j, pl.ds(0, rows), :],
            state_ref[j, pl.ds(rows, rows), :],
            state_ref[j, pl.ds(2 * rows, rows), :],
            grad_ref[out, :],
        )
        master_out[out, :] = new
        first_out[out, :] = first_new
        second_out[out, :] = second_new
        low_out[out, :] = new.astype(low_out.dtype)


def adam_from_blocks(state, grad, per=2):
    sources, stacked, cols = state.shape
    rows = stacked // 3
    block = pl.BlockSpec((per * rows, cols), lambda i: (i, 0))
    f32 = jax.ShapeDtypeStruct(grad.shape, jnp.float32)
    return pl.pallas_call(
        adam_kernel,
        grid=(sources // per,),
        in_specs=[pl.BlockSpec((per, stacked, cols), lambda i: (i, 0, 0)), block],
        out_specs=[block] * 4,
        out_shape=[f32, f32, f32, jax.ShapeDtypeStruct(grad.shape, jnp.bfloat16)],
    )(state, grad)


def pack_kernel(master_ref, first_ref, second_ref, out_ref):
    rows, width = master_ref.shape[0], out_ref.shape[2]
    for j in range(out_ref.shape[0]):
        cols = pl.ds(j * width, width)
        for k, ref in enumerate((master_ref, first_ref, second_ref)):
            out_ref[j, pl.ds(k * rows, rows), :] = ref[:, cols]


def pack_by_destination(master, first, second, dests, per=2):
    rows, cols = master.shape
    width = cols // dests
    block = pl.BlockSpec((rows, per * width), lambda i: (0, i))
    return pl.pallas_call(
        pack_kernel,
        grid=(dests // per,),
        in_specs=[block] * 3,
        out_specs=pl.BlockSpec((per, 3 * rows, width), lambda i: (i, 0, 0)),
        out_shape=jax.ShapeDtypeStruct((dests, 3 * rows, width), master.dtype),
    )(master, first, second)


def gather_rows(x, axis_name, size):
    copies = jnp.broadcast_to(x[None], (size,) + x.shape).reshape((size * x.shape[0],) + x.shape[1:])
    return lax.all_to_all(copies, axis_name, split_axis=0, concat_axis=0, tiled=True)


def scatter_sum_rows(x, axis_name, size):
    parts = lax.all_to_all(x, axis_name, split_axis=0, concat_axis=0, tiled=True)
    return parts.reshape((size, x.shape[0] // size) + x.shape[1:]).sum(axis=0)


def step(
    probe_states,
    wq_master,
    wq_first,
    wq_second,
    wq_grad,
    wkv_master,
    wkv_first,
    wkv_second,
    wkv_grad,
):
    fsdp = lax.axis_size("fsdp")
    me = lax.axis_index("fsdp")
    width = probe_states.shape[1] // fsdp
    got = [lax.dynamic_slice_in_dim(probe_states, me * width, width, 1)]
    for k in range(1, fsdp):
        block = lax.dynamic_slice_in_dim(probe_states, ((me + k) % fsdp) * width, width, 1)
        got.append(lax.ppermute(block, "fsdp", [(i, (i + k) % fsdp) for i in range(fsdp)]))
    got = jnp.stack(got[::-1])
    columns = lax.dynamic_slice_in_dim(jnp.concatenate([got, got]), fsdp - 1 - me, fsdp, 0)
    columns = columns.reshape(fsdp * probe_states.shape[0], width)
    wkv_new, wkv_mom, wkv_var = adam_step(wkv_master, wkv_first, wkv_second, wkv_grad)
    tp = lax.axis_size("tp")
    me_tp = lax.axis_index("tp")
    wkv_low = wkv_new.astype(jnp.bfloat16)
    slice_kv = wkv_low.shape[1] // tp
    rows_kv = [lax.dynamic_slice_in_dim(wkv_low, me_tp * slice_kv, slice_kv, 1)]
    for k in range(1, tp):
        block = lax.dynamic_slice_in_dim(wkv_low, ((me_tp + k) % tp) * slice_kv, slice_kv, 1)
        rows_kv.append(lax.ppermute(block, "tp", [(i, (i + k) % tp) for i in range(tp)]))
    rows_kv = jnp.stack(rows_kv[::-1])
    wkv_rows = lax.dynamic_slice_in_dim(jnp.concatenate([rows_kv, rows_kv]), tp - 1 - me_tp, tp, 0)
    wkv_rows = wkv_rows.reshape(tp * wkv_low.shape[0], slice_kv)
    kv_term = jnp.dot(columns, wkv_rows, preferred_element_type=jnp.float32)

    send = pack_by_destination(wq_master, wq_first, wq_second, tp)
    state = lax.all_to_all(send, "tp", split_axis=0, concat_axis=0, tiled=True)
    wq_new, wq_mom, wq_var, wq_low = adam_from_blocks(state, wq_grad)
    q_term = jnp.dot(columns, wq_low, preferred_element_type=jnp.float32)

    sums = scatter_sum_rows(jnp.concatenate([q_term, kv_term], axis=1), "fsdp", fsdp)
    q_cols = q_term.shape[1]
    probe_query = sums[:, :q_cols].astype(jnp.bfloat16)
    kv_block = sums[:, q_cols:].astype(jnp.bfloat16)
    kv_all = gather_rows(kv_block, ("fsdp", "tp"), fsdp * tp)
    tokens = kv_block.shape[0]
    kv_all = kv_all.reshape(fsdp, tp, tokens, slice_kv).transpose(0, 2, 1, 3)
    probe_keyvalue = kv_all.reshape(fsdp * tokens, tp * slice_kv)
    return (wq_new, wq_mom, wq_var, wkv_new, wkv_mom, wkv_var, probe_query, probe_keyvalue)


def solution(mesh):
    return jax.shard_map(
        step,
        mesh=mesh,
        in_specs=(
            P("fsdp", None),
            P(("fsdp", "tp"), None),
            P(("fsdp", "tp"), None),
            P(("fsdp", "tp"), None),
            P("fsdp", "tp"),
            P(("fsdp", "tp"), None),
            P(("fsdp", "tp"), None),
            P(("fsdp", "tp"), None),
            P(("fsdp", "tp"), None),
        ),
        out_specs=(
            P("fsdp", "tp"),
            P("fsdp", "tp"),
            P("fsdp", "tp"),
            P(("fsdp", "tp"), None),
            P(("fsdp", "tp"), None),
            P(("fsdp", "tp"), None),
            P("fsdp", "tp"),
            P(),
        ),
        check_vma=False,
    )
```

```python
import math

import jax
import jax.numpy as jnp
from jax import lax
from jax.experimental import pallas as pl
from jax.sharding import PartitionSpec as P


BETA_ONE = 0.9
BETA_TWO = 0.95
LEARN_RATE = 0.001
EPSILON = 1e-08
CORRECT_ONE = 1.0 - math.exp(1000.0 * math.log(0.9))
CORRECT_TWO = 1.0 - math.exp(1000.0 * math.log(0.95))


def adam_step(master, first, second, grad):
    first_new = BETA_ONE * first + (1.0 - BETA_ONE) * grad
    second_new = BETA_TWO * second + (1.0 - BETA_TWO) * grad * grad
    update = first_new / CORRECT_ONE / (jnp.sqrt(second_new / CORRECT_TWO) + EPSILON)
    return (master - LEARN_RATE * update, first_new, second_new)


def adam_kernel(state_ref, second_ref, grad_ref, master_out, first_out, second_out, low_out):
    per, rows = state_ref.shape[0], grad_ref.shape[0] // state_ref.shape[0]
    for j in range(per):
        out = pl.ds(j * rows, rows)
        new, first_new, second_new = adam_step(
            state_ref[j, pl.ds(0, rows), :],
            state_ref[j, pl.ds(rows, rows), :],
            second_ref[out, :],
            grad_ref[out, :],
        )
        master_out[out, :] = new
        first_out[out, :] = first_new
        second_out[out, :] = second_new
        low_out[out, :] = new.astype(low_out.dtype)


def adam_from_blocks(state, second, grad, per=2):
    sources, stacked, cols = state.shape
    rows = stacked // 2
    block = pl.BlockSpec((per * rows, cols), lambda i: (i, 0))
    f32 = jax.ShapeDtypeStruct(grad.shape, jnp.float32)
    return pl.pallas_call(
        adam_kernel,
        grid=(sources // per,),
        in_specs=[pl.BlockSpec((per, stacked, cols), lambda i: (i, 0, 0)), block, block],
        out_specs=[block] * 4,
        out_shape=[f32, f32, f32, jax.ShapeDtypeStruct(grad.shape, jnp.bfloat16)],
    )(state, second, grad)


def pack_kernel(*refs):
    *in_refs, out_ref = refs
    rows, width = in_refs[0].shape[0], out_ref.shape[2]
    for j in range(out_ref.shape[0]):
        cols = pl.ds(j * width, width)
        for k, ref in enumerate(in_refs):
            out_ref[j, pl.ds(k * rows, rows), :] = ref[:, cols]


def pack_by_destination(arrays, dests, per=2):
    rows, cols = arrays[0].shape
    width = cols // dests
    block = pl.BlockSpec((rows, per * width), lambda i: (0, i))
    return pl.pallas_call(
        pack_kernel,
        grid=(dests // per,),
        in_specs=[block] * len(arrays),
        out_specs=pl.BlockSpec((per, len(arrays) * rows, width), lambda i: (i, 0, 0)),
        out_shape=jax.ShapeDtypeStruct((dests, len(arrays) * rows, width), arrays[0].dtype),
    )(*arrays)


def gather_rows(x, axis_name, size):
    copies = jnp.broadcast_to(x[None], (size,) + x.shape).reshape((size * x.shape[0],) + x.shape[1:])
    return lax.all_to_all(copies, axis_name, split_axis=0, concat_axis=0, tiled=True)


def scatter_sum_rows(x, axis_name, size):
    parts = lax.all_to_all(x, axis_name, split_axis=0, concat_axis=0, tiled=True)
    return parts.reshape((size, x.shape[0] // size) + x.shape[1:]).sum(axis=0)


def step(
    probe_states,
    wq_master,
    wq_first,
    wq_second,
    wq_grad,
    wkv_master,
    wkv_first,
    wkv_second,
    wkv_grad,
):
    fsdp = lax.axis_size("fsdp")
    me = lax.axis_index("fsdp")
    width = probe_states.shape[1] // fsdp
    got = [lax.dynamic_slice_in_dim(probe_states, me * width, width, 1)]
    for k in range(1, fsdp):
        block = lax.dynamic_slice_in_dim(probe_states, ((me + k) % fsdp) * width, width, 1)
        got.append(lax.ppermute(block, "fsdp", [(i, (i + k) % fsdp) for i in range(fsdp)]))
    got = jnp.stack(got[::-1])
    columns = lax.dynamic_slice_in_dim(jnp.concatenate([got, got]), fsdp - 1 - me, fsdp, 0)
    columns = columns.reshape(fsdp * probe_states.shape[0], width)
    wkv_new, wkv_mom, wkv_var = adam_step(wkv_master, wkv_first, wkv_second, wkv_grad)
    tp = lax.axis_size("tp")
    me_tp = lax.axis_index("tp")
    wkv_low = wkv_new.astype(jnp.bfloat16)
    slice_kv = wkv_low.shape[1] // tp
    rows_kv = [lax.dynamic_slice_in_dim(wkv_low, me_tp * slice_kv, slice_kv, 1)]
    for k in range(1, tp):
        block = lax.dynamic_slice_in_dim(wkv_low, ((me_tp + k) % tp) * slice_kv, slice_kv, 1)
        rows_kv.append(lax.ppermute(block, "tp", [(i, (i + k) % tp) for i in range(tp)]))
    rows_kv = jnp.stack(rows_kv[::-1])
    wkv_rows = lax.dynamic_slice_in_dim(jnp.concatenate([rows_kv, rows_kv]), tp - 1 - me_tp, tp, 0)
    wkv_rows = wkv_rows.reshape(tp * wkv_low.shape[0], slice_kv)
    kv_term = jnp.dot(columns, wkv_rows, preferred_element_type=jnp.float32)

    rows, cols = wq_master.shape
    send = pack_by_destination((wq_master, wq_first), tp)
    width = cols // tp
    got2 = [lax.dynamic_slice_in_dim(wq_second, me_tp * width, width, 1)]
    state = lax.all_to_all(send, "tp", split_axis=0, concat_axis=0, tiled=True)
    for k in range(1, tp):
        block = lax.dynamic_slice_in_dim(wq_second, ((me_tp + k) % tp) * width, width, 1)
        got2.append(lax.ppermute(block, "tp", [(i, (i + k) % tp) for i in range(tp)]))
    got2 = jnp.stack(got2[::-1])
    second = lax.dynamic_slice_in_dim(jnp.concatenate([got2, got2]), tp - 1 - me_tp, tp, 0)
    second = second.reshape(tp * rows, width)
    wq_new, wq_mom, wq_var, wq_low = adam_from_blocks(state, second, wq_grad)
    q_term = jnp.dot(columns, wq_low, preferred_element_type=jnp.float32)

    sums = scatter_sum_rows(jnp.concatenate([q_term, kv_term], axis=1), "fsdp", fsdp)
    q_cols = q_term.shape[1]
    probe_query = sums[:, :q_cols].astype(jnp.bfloat16)
    kv_block = sums[:, q_cols:].astype(jnp.bfloat16)
    tokens = kv_block.shape[0]
    lanes = 128
    kv_all = gather_rows(kv_block.reshape(tokens * slice_kv // lanes, lanes), ("fsdp", "tp"), fsdp * tp)
    kv_all = kv_all.reshape(fsdp, tp, tokens, slice_kv).transpose(0, 2, 1, 3)
    probe_keyvalue = kv_all.reshape(fsdp * tokens, tp * slice_kv)
    return (wq_new, wq_mom, wq_var, wkv_new, wkv_mom, wkv_var, probe_query, probe_keyvalue)


def solution(mesh):
    return jax.shard_map(
        step,
        mesh=mesh,
        in_specs=(
            P("fsdp", None),
            P(("fsdp", "tp"), None),
            P(("fsdp", "tp"), None),
            P(("fsdp", "tp"), None),
            P("fsdp", "tp"),
            P(("fsdp", "tp"), None),
            P(("fsdp", "tp"), None),
            P(("fsdp", "tp"), None),
            P(("fsdp", "tp"), None),
        ),
        out_specs=(
            P("fsdp", "tp"),
            P("fsdp", "tp"),
            P("fsdp", "tp"),
            P(("fsdp", "tp"), None),
            P(("fsdp", "tp"), None),
            P(("fsdp", "tp"), None),
            P("fsdp", "tp"),
            P(),
        ),
        check_vma=False,
    )
```

```python
import math

import jax
import jax.numpy as jnp
from jax import lax
from jax.experimental import pallas as pl
from jax.sharding import PartitionSpec as P


BETA_ONE = 0.9
BETA_TWO = 0.95
LEARN_RATE = 0.001
EPSILON = 1e-08
CORRECT_ONE = 1.0 - math.exp(1000.0 * math.log(0.9))
CORRECT_TWO = 1.0 - math.exp(1000.0 * math.log(0.95))


def adam_step(master, first, second, grad):
    first_new = BETA_ONE * first + (1.0 - BETA_ONE) * grad
    second_new = BETA_TWO * second + (1.0 - BETA_TWO) * grad * grad
    update = first_new / CORRECT_ONE / (jnp.sqrt(second_new / CORRECT_TWO) + EPSILON)
    return (master - LEARN_RATE * update, first_new, second_new)


def adam_kernel(state_ref, grad_ref, columns_ref, master_out, first_out, second_out, low_out, q_out):
    per, rows = state_ref.shape[0], grad_ref.shape[0] // state_ref.shape[0]

    @pl.when(pl.program_id(0) == 0)
    def _():
        q_out[...] = jnp.zeros_like(q_out)

    for j in range(per):
        out = pl.ds(j * rows, rows)
        new, first_new, second_new = adam_step(
            state_ref[j, pl.ds(0, rows), :],
            state_ref[j, pl.ds(rows, rows), :],
            state_ref[j, pl.ds(2 * rows, rows), :],
            grad_ref[out, :],
        )
        master_out[out, :] = new
        first_out[out, :] = first_new
        second_out[out, :] = second_new
        low = new.astype(low_out.dtype)
        low_out[out, :] = low
        q_out[...] += jnp.dot(columns_ref[:, out], low, preferred_element_type=jnp.float32)


def adam_from_blocks(state, grad, columns, per=2):
    sources, stacked, cols = state.shape
    rows = stacked // 3
    block = pl.BlockSpec((per * rows, cols), lambda i: (i, 0))
    f32 = jax.ShapeDtypeStruct(grad.shape, jnp.float32)
    return pl.pallas_call(
        adam_kernel,
        grid=(sources // per,),
        in_specs=[
            pl.BlockSpec((per, stacked, cols), lambda i: (i, 0, 0)),
            block,
            pl.BlockSpec((columns.shape[0], per * rows), lambda i: (0, i)),
        ],
        out_specs=[block] * 4 + [pl.BlockSpec((columns.shape[0], cols), lambda i: (0, 0))],
        out_shape=[f32, f32, f32, jax.ShapeDtypeStruct(grad.shape, jnp.bfloat16),
                   jax.ShapeDtypeStruct((columns.shape[0], cols), jnp.float32)],
    )(state, grad, columns)


def pack_kernel(master_ref, first_ref, second_ref, out_ref):
    rows, width = master_ref.shape[0], out_ref.shape[2]
    for j in range(out_ref.shape[0]):
        cols = pl.ds(j * width, width)
        for k, ref in enumerate((master_ref, first_ref, second_ref)):
            out_ref[j, pl.ds(k * rows, rows), :] = ref[:, cols]


def pack_by_destination(master, first, second, dests, per=2):
    rows, cols = master.shape
    width = cols // dests
    block = pl.BlockSpec((rows, per * width), lambda i: (0, i))
    return pl.pallas_call(
        pack_kernel,
        grid=(dests // per,),
        in_specs=[block] * 3,
        out_specs=pl.BlockSpec((per, 3 * rows, width), lambda i: (i, 0, 0)),
        out_shape=jax.ShapeDtypeStruct((dests, 3 * rows, width), master.dtype),
    )(master, first, second)


def gather_rows(x, axis_name, size):
    copies = jnp.broadcast_to(x[None], (size,) + x.shape).reshape((size * x.shape[0],) + x.shape[1:])
    return lax.all_to_all(copies, axis_name, split_axis=0, concat_axis=0, tiled=True)


def scatter_sum_rows(x, axis_name, size):
    parts = lax.all_to_all(x, axis_name, split_axis=0, concat_axis=0, tiled=True)
    return parts.reshape((size, x.shape[0] // size) + x.shape[1:]).sum(axis=0)


def step(
    probe_states,
    wq_master,
    wq_first,
    wq_second,
    wq_grad,
    wkv_master,
    wkv_first,
    wkv_second,
    wkv_grad,
):
    fsdp = lax.axis_size("fsdp")
    me = lax.axis_index("fsdp")
    width = probe_states.shape[1] // fsdp
    got = [lax.dynamic_slice_in_dim(probe_states, me * width, width, 1)]
    for k in range(1, fsdp):
        block = lax.dynamic_slice_in_dim(probe_states, ((me + k) % fsdp) * width, width, 1)
        got.append(lax.ppermute(block, "fsdp", [(i, (i + k) % fsdp) for i in range(fsdp)]))
    got = jnp.stack(got[::-1])
    columns = lax.dynamic_slice_in_dim(jnp.concatenate([got, got]), fsdp - 1 - me, fsdp, 0)
    columns = columns.reshape(fsdp * probe_states.shape[0], width)
    wkv_new, wkv_mom, wkv_var = adam_step(wkv_master, wkv_first, wkv_second, wkv_grad)
    tp = lax.axis_size("tp")
    me_tp = lax.axis_index("tp")
    wkv_low = wkv_new.astype(jnp.bfloat16)
    slice_kv = wkv_low.shape[1] // tp
    rows_kv = [lax.dynamic_slice_in_dim(wkv_low, me_tp * slice_kv, slice_kv, 1)]
    for k in range(1, tp):
        block = lax.dynamic_slice_in_dim(wkv_low, ((me_tp + k) % tp) * slice_kv, slice_kv, 1)
        rows_kv.append(lax.ppermute(block, "tp", [(i, (i + k) % tp) for i in range(tp)]))
    rows_kv = jnp.stack(rows_kv[::-1])
    wkv_rows = lax.dynamic_slice_in_dim(jnp.concatenate([rows_kv, rows_kv]), tp - 1 - me_tp, tp, 0)
    wkv_rows = wkv_rows.reshape(tp * wkv_low.shape[0], slice_kv)
    kv_term = jnp.dot(columns, wkv_rows, preferred_element_type=jnp.float32)

    send = pack_by_destination(wq_master, wq_first, wq_second, tp)
    state = lax.all_to_all(send, "tp", split_axis=0, concat_axis=0, tiled=True)
    wq_new, wq_mom, wq_var, _, q_term = adam_from_blocks(state, wq_grad, columns)

    sums = scatter_sum_rows(jnp.concatenate([q_term, kv_term], axis=1), "fsdp", fsdp)
    q_cols = q_term.shape[1]
    probe_query = sums[:, :q_cols].astype(jnp.bfloat16)
    kv_block = sums[:, q_cols:].astype(jnp.bfloat16)
    tokens = kv_block.shape[0]
    lanes = 128
    kv_all = gather_rows(kv_block.reshape(tokens * slice_kv // lanes, lanes), ("fsdp", "tp"), fsdp * tp)
    kv_all = kv_all.reshape(fsdp, tp, tokens, slice_kv).transpose(0, 2, 1, 3)
    probe_keyvalue = kv_all.reshape(fsdp * tokens, tp * slice_kv)
    return (wq_new, wq_mom, wq_var, wkv_new, wkv_mom, wkv_var, probe_query, probe_keyvalue)


def solution(mesh):
    return jax.shard_map(
        step,
        mesh=mesh,
        in_specs=(
            P("fsdp", None),
            P(("fsdp", "tp"), None),
            P(("fsdp", "tp"), None),
            P(("fsdp", "tp"), None),
            P("fsdp", "tp"),
            P(("fsdp", "tp"), None),
            P(("fsdp", "tp"), None),
            P(("fsdp", "tp"), None),
            P(("fsdp", "tp"), None),
        ),
        out_specs=(
            P("fsdp", "tp"),
            P("fsdp", "tp"),
            P("fsdp", "tp"),
            P(("fsdp", "tp"), None),
            P(("fsdp", "tp"), None),
            P(("fsdp", "tp"), None),
            P("fsdp", "tp"),
            P(),
        ),
        check_vma=False,
    )
```

```python
import math

import jax
import jax.numpy as jnp
from jax import lax
from jax.experimental import pallas as pl
from jax.sharding import PartitionSpec as P


BETA_ONE = 0.9
BETA_TWO = 0.95
LEARN_RATE = 0.001
EPSILON = 1e-08
CORRECT_ONE = 1.0 - math.exp(1000.0 * math.log(0.9))
CORRECT_TWO = 1.0 - math.exp(1000.0 * math.log(0.95))


def adam_step(master, first, second, grad):
    first_new = BETA_ONE * first + (1.0 - BETA_ONE) * grad
    second_new = BETA_TWO * second + (1.0 - BETA_TWO) * grad * grad
    update = first_new / CORRECT_ONE / (jnp.sqrt(second_new / CORRECT_TWO) + EPSILON)
    return (master - LEARN_RATE * update, first_new, second_new)


def adam_kernel(state_ref, grad_ref, master_out, first_out, second_out, low_out):
    per, rows = state_ref.shape[0], grad_ref.shape[0] // state_ref.shape[0]
    for j in range(per):
        out = pl.ds(j * rows, rows)
        new, first_new, second_new = adam_step(
            state_ref[j, pl.ds(0, rows), :],
            state_ref[j, pl.ds(rows, rows), :],
            state_ref[j, pl.ds(2 * rows, rows), :],
            grad_ref[out, :],
        )
        master_out[out, :] = new
        first_out[out, :] = first_new
        second_out[out, :] = second_new
        low_out[out, :] = new.astype(low_out.dtype)


def adam_from_blocks(state, grad, per=4):
    sources, stacked, cols = state.shape
    rows = stacked // 3
    block = pl.BlockSpec((per * rows, cols), lambda i: (i, 0))
    f32 = jax.ShapeDtypeStruct(grad.shape, jnp.float32)
    return pl.pallas_call(
        adam_kernel,
        grid=(sources // per,),
        in_specs=[pl.BlockSpec((per, stacked, cols), lambda i: (i, 0, 0)), block],
        out_specs=[block] * 4,
        out_shape=[f32, f32, f32, jax.ShapeDtypeStruct(grad.shape, jnp.bfloat16)],
    )(state, grad)


def pack_kernel(master_ref, first_ref, second_ref, out_ref):
    rows, width = master_ref.shape[0], out_ref.shape[2]
    for j in range(out_ref.shape[0]):
        cols = pl.ds(j * width, width)
        for k, ref in enumerate((master_ref, first_ref, second_ref)):
            out_ref[j, pl.ds(k * rows, rows), :] = ref[:, cols]


def pack_by_destination(master, first, second, dests, per=4):
    rows, cols = master.shape
    width = cols // dests
    block = pl.BlockSpec((rows, per * width), lambda i: (0, i))
    return pl.pallas_call(
        pack_kernel,
        grid=(dests // per,),
        in_specs=[block] * 3,
        out_specs=pl.BlockSpec((per, 3 * rows, width), lambda i: (i, 0, 0)),
        out_shape=jax.ShapeDtypeStruct((dests, 3 * rows, width), master.dtype),
    )(master, first, second)


def gather_rows(x, axis_name, size):
    copies = jnp.broadcast_to(x[None], (size,) + x.shape).reshape((size * x.shape[0],) + x.shape[1:])
    return lax.all_to_all(copies, axis_name, split_axis=0, concat_axis=0, tiled=True)


def scatter_sum_rows(x, axis_name, size):
    parts = lax.all_to_all(x, axis_name, split_axis=0, concat_axis=0, tiled=True)
    return parts.reshape((size, x.shape[0] // size) + x.shape[1:]).sum(axis=0)


def step(
    probe_states,
    wq_master,
    wq_first,
    wq_second,
    wq_grad,
    wkv_master,
    wkv_first,
    wkv_second,
    wkv_grad,
):
    fsdp = lax.axis_size("fsdp")
    me = lax.axis_index("fsdp")
    width = probe_states.shape[1] // fsdp
    got = [lax.dynamic_slice_in_dim(probe_states, me * width, width, 1)]
    for k in range(1, fsdp):
        block = lax.dynamic_slice_in_dim(probe_states, ((me + k) % fsdp) * width, width, 1)
        got.append(lax.ppermute(block, "fsdp", [(i, (i + k) % fsdp) for i in range(fsdp)]))
    got = jnp.stack(got[::-1])
    columns = lax.dynamic_slice_in_dim(jnp.concatenate([got, got]), fsdp - 1 - me, fsdp, 0)
    columns = columns.reshape(fsdp * probe_states.shape[0], width)
    wkv_new, wkv_mom, wkv_var = adam_step(wkv_master, wkv_first, wkv_second, wkv_grad)
    tp = lax.axis_size("tp")
    me_tp = lax.axis_index("tp")
    wkv_low = wkv_new.astype(jnp.bfloat16)
    slice_kv = wkv_low.shape[1] // tp
    rows_kv = [lax.dynamic_slice_in_dim(wkv_low, me_tp * slice_kv, slice_kv, 1)]
    for k in range(1, tp):
        block = lax.dynamic_slice_in_dim(wkv_low, ((me_tp + k) % tp) * slice_kv, slice_kv, 1)
        rows_kv.append(lax.ppermute(block, "tp", [(i, (i + k) % tp) for i in range(tp)]))
    rows_kv = jnp.stack(rows_kv[::-1])
    wkv_rows = lax.dynamic_slice_in_dim(jnp.concatenate([rows_kv, rows_kv]), tp - 1 - me_tp, tp, 0)
    wkv_rows = wkv_rows.reshape(tp * wkv_low.shape[0], slice_kv)
    kv_term = jnp.dot(columns, wkv_rows, preferred_element_type=jnp.float32)

    send = pack_by_destination(wq_master, wq_first, wq_second, tp)
    state = lax.all_to_all(send, "tp", split_axis=0, concat_axis=0, tiled=True)
    wq_new, wq_mom, wq_var, wq_low = adam_from_blocks(state, wq_grad)
    q_term = jnp.dot(columns, wq_low, preferred_element_type=jnp.float32)

    sums = scatter_sum_rows(jnp.concatenate([q_term, kv_term], axis=1), "fsdp", fsdp)
    q_cols = q_term.shape[1]
    probe_query = sums[:, :q_cols].astype(jnp.bfloat16)
    kv_block = sums[:, q_cols:].astype(jnp.bfloat16)
    tokens = kv_block.shape[0]
    lanes = 128
    kv_all = gather_rows(kv_block.reshape(tokens * slice_kv // lanes, lanes), ("fsdp", "tp"), fsdp * tp)
    kv_all = kv_all.reshape(fsdp, tp, tokens, slice_kv).transpose(0, 2, 1, 3)
    probe_keyvalue = kv_all.reshape(fsdp * tokens, tp * slice_kv)
    return (wq_new, wq_mom, wq_var, wkv_new, wkv_mom, wkv_var, probe_query, probe_keyvalue)


def solution(mesh):
    return jax.shard_map(
        step,
        mesh=mesh,
        in_specs=(
            P("fsdp", None),
            P(("fsdp", "tp"), None),
            P(("fsdp", "tp"), None),
            P(("fsdp", "tp"), None),
            P("fsdp", "tp"),
            P(("fsdp", "tp"), None),
            P(("fsdp", "tp"), None),
            P(("fsdp", "tp"), None),
            P(("fsdp", "tp"), None),
        ),
        out_specs=(
            P("fsdp", "tp"),
            P("fsdp", "tp"),
            P("fsdp", "tp"),
            P(("fsdp", "tp"), None),
            P(("fsdp", "tp"), None),
            P(("fsdp", "tp"), None),
            P("fsdp", "tp"),
            P(),
        ),
        check_vma=False,
    )
```
